32 devices in a mesh: dp: 8 (over z, x), rows: 4 (over y, core).
Axes of the slice: x: 2, y: 2, z: 4, core: 2. Of those that a mesh axis runs over, the one named last changes fastest.
Arguments:
- token_ids: int32 [32, 128], P(('dp', 'rows')), may hold values from 0 to 4095, as said below
- upstream: bfloat16 [32, 128, 5376], P(('dp', 'rows')), may hold values from -6 to 6
- saved_rows: bfloat16 [32, 128, 5376], P(('dp', 'rows')), may hold values from -4 to 4
- norm_gain: float32 [5376], replicated, may hold values from 0.5 to 1.5
- master: float32 [4096, 5376], P('rows', 'dp'), may hold values from -6 to 6
- moment_one: float32 [4096, 5376], P('rows', 'dp'), may hold values from -4 to 4
- moment_two: float32 [4096, 5376], P('rows', 'dp'), may hold values from 0.1 to 4
Outputs:
- master_new: float32 [4096, 5376], P('rows', 'dp')
- moment_one_new: float32 [4096, 5376], P('rows', 'dp')
- moment_two_new: float32 [4096, 5376], P('rows', 'dp')
- new_rows: bfloat16 [32, 128, 5376], P(('dp', 'rows'))
The draws below stay inside these ranges and needn't reach their ends.
Inputs may be any that keep to these rules, and one draw needn't show every extreme that they name: `token_ids`: rows v with v // 1024 = k belong to owner k. In each sequence, one owner receives exactly 32 of its tokens and every other owner at most 32.
All inputs are finite; a program needn't handle non-finite values.
Results may differ from the reference program's by a relative error of at most 0.007.
Values may be sent and summed in bfloat16 or wider, within the bound.
No kernel may reach another device: no remote copies, remote signals or barrier semaphores. Data moves between devices by JAX's collectives and lax.ppermute only.
A program may use at most 64 MiB of HBM per device.

```python
import math
import jax
import jax.numpy as jnp
from jax import lax

D = 5376
TOK = 128
VROWS_DEV = 1024
SEQS = 32
VOCAB = 4096
N_ROWS = 4


def draw_token_ids(key, part):
    hot_count = TOK // 4
    keys = jax.random.split(jax.random.fold_in(key, 7), 5)
    hot_owner = jax.random.randint(keys[0], (SEQS, 1), 0, N_ROWS)
    position = jnp.arange(TOK, dtype=jnp.int32)[None, :]
    offset = jnp.where(position < hot_count, 0, 1 + (position - hot_count) % (N_ROWS - 1))
    owner = (hot_owner + offset) % N_ROWS
    scores = jax.random.randint(keys[1], (SEQS, TOK), 0, 65536) * TOK + position
    order = jnp.argsort(scores, axis=1, stable=True)
    owner = jnp.take_along_axis(owner, order, axis=1)
    first = jax.random.randint(keys[2], (SEQS, TOK), 0, VROWS_DEV)
    second = jax.random.randint(keys[3], (SEQS, TOK), 0, VROWS_DEV)
    skewed = first * second // VROWS_DEV
    shuffle = jax.random.permutation(keys[4], VROWS_DEV).astype(jnp.int32)
    local = jnp.take(shuffle, skewed, axis=0)
    return (owner * VROWS_DEV + local).astype(jnp.int32)


def steps_of(stream_key, extent, cuts, low, high):
    def one(dim, parts):
        draws = jax.random.uniform(jax.random.fold_in(jax.random.fold_in(stream_key, 6), dim), (parts,), jnp.float32, low / len(cuts), high / len(cuts))
        return jnp.repeat(jnp.exp(draws), extent[dim] // parts).reshape((-1,) + (1,) * (len(extent) - dim - 1))

    loudness = one(*cuts[0])
    for cut in cuts[1:]:
        loudness = loudness * one(*cut)
    return loudness


def gaussian(rng, shape, deviation, most, shards=(), kind=jnp.bfloat16):
    entries = jax.random.normal(rng, shape, jnp.float32) * deviation
    if len(shards) > 0:
        entries = steps_of(rng, shape, shards, -0.22, 0.18) * entries
    return jnp.clip(entries, min=-most, max=most).astype(kind)


def setup_inputs(seed: int = 0) -> dict:
    seeds = jax.random.split(jax.random.key(seed), 8)
    token_ids = draw_token_ids(jax.random.fold_in(seeds[7], 71), 0)
    upstream = gaussian(seeds[1], (SEQS, TOK, D), 1.0, 6.0, ((0, 32),))
    saved_rows = gaussian(seeds[2], (SEQS, TOK, D), 0.5, 4.0, ((0, 32),))
    norm_gain = jnp.clip(1.0 + 0.1 * jax.random.normal(seeds[3], (D,), jnp.float32), 0.5, 1.5)
    master = gaussian(seeds[4], (VOCAB, D), 1.0, 6.0, ((0, 4), (1, 8)), jnp.float32)
    moment_one = gaussian(seeds[5], (VOCAB, D), 0.5, 4.0, ((0, 4), (1, 8)), jnp.float32)
    moment_two = jnp.clip(jnp.exp(math.log(4.0) - 3.6888794 * jax.random.uniform(seeds[6], (VOCAB, D), jnp.float32) ** steps_of(seeds[6], (VOCAB, D), ((0, 4), (1, 8)), -0.2, 0.2)), 0.1, 4.0)
    return dict(token_ids=token_ids, upstream=upstream, saved_rows=saved_rows, norm_gain=norm_gain, master=master, moment_one=moment_one, moment_two=moment_two)


def norm_back(upstream_rows, saved, gain):
    values = saved.astype(jnp.float32)
    row_mean = lax.optimization_barrier(jnp.mean(values, axis=-1, keepdims=True))
    centered = values - row_mean
    variance = lax.optimization_barrier(jnp.mean(centered * centered, axis=-1, keepdims=True))
    inv_std = lax.rsqrt(variance + 1e-05)
    normed = centered * inv_std
    scaled = upstream_rows.astype(jnp.float32) * gain
    mean_scaled = lax.optimization_barrier(jnp.mean(scaled, axis=-1, keepdims=True))
    mean_cross = lax.optimization_barrier(jnp.mean(scaled * normed, axis=-1, keepdims=True))
    return (inv_std * (scaled - mean_scaled - normed * mean_cross)).astype(jnp.bfloat16)

def reference(token_ids, upstream, saved_rows, norm_gain, master, moment_one, moment_two):
    vocab_rows = master.shape[0]

    def seq_grad(running, sequence):
        seq_ids, seq_up, seq_saved = sequence
        row_input = norm_back(seq_up, seq_saved, norm_gain)
        added = jax.ops.segment_sum(row_input.astype(jnp.float32), seq_ids, num_segments=vocab_rows)
        return (running + added, None)
    start_grad = jnp.zeros(master.shape, jnp.float32)
    row_grad, _ = lax.scan(seq_grad, start_grad, (token_ids, upstream, saved_rows))
    moment_one_new = 0.9 * moment_one + 0.1 * row_grad
    moment_two_new = 0.999 * moment_two + 0.001 * row_grad * row_grad
    first_fix = 1.0 - 0.9 ** 10
    second_fix = 1.0 - 0.999 ** 10
    update = moment_one_new / first_fix / (jnp.sqrt(moment_two_new / second_fix) + 1e-08) + 0.1 * master
    master_new = master - 0.05 * update
    new_rows = jnp.take(master_new.astype(jnp.bfloat16), token_ids, axis=0)
    return (master_new, moment_one_new, moment_two_new, new_rows)
```

```python
import functools

import jax
import jax.numpy as jnp
from jax import lax
from jax.experimental import pallas as pl
from jax.experimental.pallas import tpu as pltpu
from jax.sharding import PartitionSpec as P

LANES = 128
F32 = jnp.float32
BF16 = jnp.bfloat16


def round_up(n, m):
    return (n + m - 1) // m * m


def dot(a, b, dims):
    return lax.dot_general(a, b, (dims, ((), ())), preferred_element_type=F32)


def swap_matrix(groups, width):
    size = groups * groups * width
    row = lax.broadcasted_iota(jnp.int32, (size, size), 0)
    col = lax.broadcasted_iota(jnp.int32, (1, size), 1)
    first = lax.div(col, groups * width)
    rest = col - first * (groups * width)
    second = lax.div(rest, width)
    target = second * (groups * width) + first * width + (rest - second * width)
    return (row == target).astype(F32).astype(BF16)


def send_kernel(
    dims, ids_ref, upstream_ref, saved_ref, gain_ref, out_ref, slots_ref, grad, turned, stacked
):
    n_dp, owners, rows_owned, capacity, base = dims
    step = pl.program_id(0)
    tile, width = upstream_ref.shape
    tokens = grad.shape[0]
    values = saved_ref[...].astype(F32)
    scaled = upstream_ref[...].astype(F32) * gain_ref[...]
    centered = values - jnp.sum(values, axis=1, keepdims=True) * (1.0 / width)
    variance = jnp.sum(centered * centered, axis=1, keepdims=True) * (1.0 / width)
    inv_std = lax.rsqrt(variance + 1e-05)
    mean_scaled = jnp.sum(scaled, axis=1, keepdims=True) * (1.0 / width)
    mean_cross = inv_std * jnp.sum(scaled * centered, axis=1, keepdims=True) * (1.0 / width)
    out = inv_std * (scaled - mean_scaled - centered * (inv_std * mean_cross))
    grad[pl.ds(pl.multiple_of(step * tile, tile), tile), :] = out.astype(BF16)

    @pl.when(step == pl.num_programs(0) - 1)
    def _():
        groups = LANES // capacity
        slots = owners * capacity
        slice_width = width // n_dp
        quarter = slice_width // groups
        block = stacked.shape[0] // (n_dp * (owners // groups))
        ids = ids_ref[...]
        owner = jnp.zeros_like(ids)
        for k in range(1, owners):
            owner = owner + (ids >= k * rows_owned).astype(jnp.int32)
        local = ids - owner * rows_owned
        down = lax.broadcasted_iota(jnp.int32, (tokens, tokens), 0)
        across = lax.broadcasted_iota(jnp.int32, (tokens, tokens), 1)
        column = lambda v: jnp.sum(
            jnp.where(down == across, jnp.broadcast_to(v.astype(F32), (tokens, tokens)), 0.0),
            axis=1,
            keepdims=True,
        )
        owner_col = column(owner)
        local_col = column(local)
        earlier = (owner.astype(F32) == owner_col) & (across < down)
        rank = jnp.sum(earlier.astype(F32), axis=1, keepdims=True)
        target = (owner_col * capacity + rank).astype(jnp.int32)
        placed = target == lax.broadcasted_iota(jnp.int32, (tokens, slots), 1)
        slot_of = placed.astype(F32).astype(BF16)
        slots_ref[...] = slot_of
        slot_id = (
            jnp.sum(jnp.where(placed, local_col + 1.0, 0.0), axis=0, keepdims=True).astype(
                jnp.int32
            )
            - 1
        )
        high = lax.shift_right_arithmetic(slot_id, base)
        low = slot_id - lax.shift_left(high, base)
        high, low = high.astype(F32), low.astype(F32)
        for k in range(width // LANES):
            turned[k * LANES : (k + 1) * LANES, :] = dot(
                grad[:, k * LANES : (k + 1) * LANES], slot_of, ((0,), (0,))
            )
        tail = block - quarter
        for q in range(owners // groups):
            lanes = slice(q * LANES, (q + 1) * LANES)
            for d in range(n_dp):
                at = (q * n_dp + d) * block
                for j in range(groups):
                    start = d * slice_width + j * quarter
                    part = turned[start : start + quarter, lanes]
                    extra = (high, low)[j][:, lanes] if j < 2 else jnp.zeros((1, LANES), F32)
                    full = jnp.concatenate(
                        [part, jnp.broadcast_to(extra, (tail, LANES))], axis=0
                    ).astype(BF16)
                    stacked[at : at + block, j * LANES : (j + 1) * LANES] = full
        swapped = dot(stacked[...], swap_matrix(groups, capacity), ((1,), (0,))).astype(BF16)
        sent = out_ref.shape[1]
        for q in range(owners // groups):
            for d in range(n_dp):
                at = (q * n_dp + d) * block
                for b in range(groups):
                    out_ref[d * owners + q * groups + b] = swapped[
                        at : at + sent, b * LANES : (b + 1) * LANES
                    ]


def update_kernel(
    dims,
    arrived_ref,
    master_hbm,
    one_hbm,
    two_hbm,
    master_out,
    one_out,
    two_out,
    out_ref,
    master,
    one,
    two,
    stacked,
    turned,
    hot,
    in_sems,
    out_sems,
):
    capacity, base = dims
    groups = LANES // capacity
    sources, sent, _ = arrived_ref.shape
    slice_width, rows_owned = master.shape
    quarter = slice_width // groups
    tiles = sources // groups
    block = stacked.shape[0] // tiles
    received = sources * capacity
    hbm_in = (master_hbm, one_hbm, two_hbm)
    hbm_out = (master_out, one_out, two_out)
    held = (master, one, two)

    pieces = in_sems.shape[1]
    height = slice_width // pieces

    def copies(sources, targets, sems):
        return [
            [
                pltpu.make_async_copy(
                    source.at[p * height : (p + 1) * height, :],
                    target.at[p * height : (p + 1) * height, :],
                    sems.at[i, p],
                )
                for i, (source, target) in enumerate(zip(sources, targets))
            ]
            for p in range(pieces)
        ]

    loads = copies(hbm_in, held, in_sems)
    stores = copies(held, hbm_out, out_sems)
    for piece in loads:
        for copy in piece:
            copy.start()
    swap = swap_matrix(groups, capacity)
    for a in range(tiles):
        for b in range(groups):
            stacked[a * block : a * block + sent, b * LANES : (b + 1) * LANES] = arrived_ref[
                a * groups + b
            ]
    swapped = dot(stacked[...], swap, ((1,), (0,)))
    down = lax.broadcasted_iota(jnp.int32, (rows_owned, LANES), 0)
    for a in range(tiles):
        lanes = slice(a * LANES, (a + 1) * LANES)
        at = a * block
        for j in range(groups):
            turned[j * block : (j + 1) * block, lanes] = swapped[
                at : at + block, j * LANES : (j + 1) * LANES
            ].astype(BF16)
        id_row = sent - 1
        high = swapped[at + id_row : at + id_row + 1, 0:LANES].astype(jnp.int32)
        low = swapped[at + id_row : at + id_row + 1, LANES : 2 * LANES].astype(jnp.int32)
        ids = lax.shift_left(high, base) + low
        hot[:, lanes] = (down == ids).astype(F32).astype(BF16)
    first_fix = 1.0 - 0.9**10
    second_fix = 1.0 - 0.999**10
    for j in range(groups):
        total = dot(turned[j * block : (j + 1) * block, :], hot[...], ((1,), (1,)))[:quarter]
        if j < pieces:
            for copy in loads[j]:
                copy.wait()
        rows = slice(j * quarter, (j + 1) * quarter)
        old = master[rows, :]
        first = 0.9 * one[rows, :] + 0.1 * total
        second = 0.999 * two[rows, :] + 0.001 * total * total
        update = first / first_fix / (jnp.sqrt(second / second_fix) + 1e-08) + 0.1 * old
        new = old - 0.05 * update
        master[rows, :] = new
        one[rows, :] = first
        two[rows, :] = second
        if j >= groups - pieces:
            for copy in stores[j - (groups - pieces)]:
                copy.start()
        looked = dot(new.astype(BF16), hot[...], ((1,), (0,))).astype(BF16)
        for a in range(tiles):
            stacked[a * block : a * block + quarter, j * LANES : (j + 1) * LANES] = looked[
                :, a * LANES : (a + 1) * LANES
            ]
    back = dot(stacked[...], swap, ((1,), (0,))).astype(BF16)
    for a in range(tiles):
        for b in range(groups):
            out_ref[a * groups + b] = back[
                a * block : a * block + quarter, b * LANES : (b + 1) * LANES
            ]
    for piece in stores:
        for copy in piece:
            copy.wait()


def place_kernel(dims, rows_ref, slots_ref, out_ref, stacked, turned):
    n_dp, owners, capacity = dims
    groups = LANES // capacity
    quarter = rows_ref.shape[1]
    width = out_ref.shape[1]
    slice_width = width // n_dp
    block = stacked.shape[0] // (n_dp * (owners // groups))
    for q in range(owners // groups):
        for d in range(n_dp):
            at = (q * n_dp + d) * block
            for b in range(groups):
                stacked[at : at + quarter, b * LANES : (b + 1) * LANES] = rows_ref[
                    d * owners + q * groups + b
                ]
    swapped = dot(stacked[...], swap_matrix(groups, capacity), ((1,), (0,)))
    for q in range(owners // groups):
        for d in range(n_dp):
            at = (q * n_dp + d) * block
            for j in range(groups):
                start = d * slice_width + j * quarter
                turned[start : start + quarter, q * LANES : (q + 1) * LANES] = swapped[
                    at : at + quarter, j * LANES : (j + 1) * LANES
                ]
    for k in range(width // LANES):
        lanes = slice(k * LANES, (k + 1) * LANES)
        out_ref[:, lanes] = dot(
            slots_ref[...], turned[lanes, :].astype(BF16), ((1,), (1,))
        ).astype(BF16)


def per_device(token_ids, upstream, saved_rows, norm_gain, master, moment_one, moment_two):
    axes = ("dp", "rows")
    n_dp, owners = lax.axis_size("dp"), lax.axis_size("rows")
    devices = n_dp * owners
    _, tokens, width = upstream.shape
    rows_owned, slice_width = master.shape
    capacity = tokens // 4
    groups = LANES // capacity
    quarter = slice_width // groups
    sent = round_up(quarter, 8) + 8
    pieces = groups if quarter % 8 == 0 else 1
    block = round_up(sent, 16)
    slots = owners * capacity
    stack = devices // groups * block
    tile = 16
    base = 7
    full = pl.BlockSpec(memory_space=pltpu.VMEM)
    hbm = pl.BlockSpec(memory_space=pl.ANY)
    blocks, slot_of = pl.pallas_call(
        functools.partial(send_kernel, (n_dp, owners, rows_owned, capacity, base)),
        grid=(tokens // tile,),
        in_specs=[
            pl.BlockSpec((1, tokens), lambda i: (0, 0)),
            pl.BlockSpec((tile, width), lambda i: (i, 0)),
            pl.BlockSpec((tile, width), lambda i: (i, 0)),
            pl.BlockSpec((1, width), lambda i: (0, 0)),
        ],
        out_specs=[
            pl.BlockSpec((devices, sent, LANES), lambda i: (0, 0, 0)),
            pl.BlockSpec((tokens, slots), lambda i: (0, 0)),
        ],
        out_shape=[
            jax.ShapeDtypeStruct((devices, sent, LANES), BF16),
            jax.ShapeDtypeStruct((tokens, slots), BF16),
        ],
        scratch_shapes=[
            pltpu.VMEM((tokens, width), BF16),
            pltpu.VMEM((width, slots), F32),
            pltpu.VMEM((stack, groups * LANES), BF16),
        ],
        name="send",
    )(token_ids, upstream[0], saved_rows[0], norm_gain[None])
    arrived = lax.all_to_all(blocks, axes, split_axis=0, concat_axis=0, tiled=True)
    state = jax.ShapeDtypeStruct((slice_width, rows_owned), F32)
    master_new, one_new, two_new, found = pl.pallas_call(
        functools.partial(update_kernel, (capacity, base)),
        in_specs=[full, hbm, hbm, hbm],
        out_specs=[hbm, hbm, hbm, full],
        out_shape=[state, state, state, jax.ShapeDtypeStruct((devices, quarter, LANES), BF16)],
        scratch_shapes=[
            pltpu.VMEM(state.shape, F32),
            pltpu.VMEM(state.shape, F32),
            pltpu.VMEM(state.shape, F32),
            pltpu.VMEM((stack, groups * LANES), BF16),
            pltpu.VMEM((groups * block, devices * capacity), BF16),
            pltpu.VMEM((rows_owned, devices * capacity), BF16),
            pltpu.SemaphoreType.DMA((3, pieces)),
            pltpu.SemaphoreType.DMA((3, pieces)),
        ],
        name="update",
    )(arrived, master.T, moment_one.T, moment_two.T)
    rows = lax.all_to_all(found, axes, split_axis=0, concat_axis=0, tiled=True)
    new_rows = pl.pallas_call(
        functools.partial(place_kernel, (n_dp, owners, capacity)),
        in_specs=[full, full],
        out_specs=full,
        out_shape=jax.ShapeDtypeStruct((tokens, width), BF16),
        scratch_shapes=[
            pltpu.VMEM((stack, groups * LANES), BF16),
            pltpu.VMEM((width, slots), F32),
        ],
        name="place",
    )(rows, slot_of)
    return (master_new.T, one_new.T, two_new.T, new_rows[None])


def solution(mesh):
    split = P(("dp", "rows"), None, None)
    slab = P("rows", "dp")
    return jax.shard_map(
        per_device,
        mesh=mesh,
        in_specs=(P(("dp", "rows"), None), split, split, P(), slab, slab, slab),
        out_specs=(slab, slab, slab, split),
        check_vma=False,
    )
```

```python
import functools

import jax
import jax.numpy as jnp
from jax import lax
from jax.experimental import pallas as pl
from jax.experimental.pallas import tpu as pltpu
from jax.sharding import PartitionSpec as P

LANES = 128
F32 = jnp.float32
BF16 = jnp.bfloat16


def round_up(n, m):
    return (n + m - 1) // m * m


def dot(a, b, dims):
    return lax.dot_general(a, b, (dims, ((), ())), preferred_element_type=F32)


def swap_matrix(groups, width):
    size = groups * groups * width
    row = lax.broadcasted_iota(jnp.int32, (size, size), 0)
    col = lax.broadcasted_iota(jnp.int32, (1, size), 1)
    first = lax.div(col, groups * width)
    rest = col - first * (groups * width)
    second = lax.div(rest, width)
    target = second * (groups * width) + first * width + (rest - second * width)
    return (row == target).astype(F32).astype(BF16)


def send_kernel(
    dims,
    ids_hbm,
    upstream_hbm,
    saved_hbm,
    gain_hbm,
    out_ref,
    slots_ref,
    ids_ref,
    gain_ref,
    upstream,
    saved,
    values,
    scaled,
    stats,
    turned,
    stacked,
    sems,
    small_sems,
):
    n_dp, owners, rows_owned, capacity, base = dims
    tokens, width = values.shape
    tile = tokens // sems.shape[1]
    columns = [slice(k * LANES, (k + 1) * LANES) for k in range(width // LANES)]
    zero = jnp.zeros((tile, LANES), F32)

    def part(step):
        return pl.ds(pl.multiple_of(step * tile, tile), tile)

    def copies(step):
        return (
            pltpu.make_async_copy(saved_hbm.at[part(step)], saved.at[part(step)], sems.at[0, step]),
            pltpu.make_async_copy(
                upstream_hbm.at[part(step)], upstream.at[part(step)], sems.at[1, step]
            ),
        )

    gain_copy = pltpu.make_async_copy(gain_hbm, gain_ref, small_sems.at[0])
    ids_copy = pltpu.make_async_copy(ids_hbm, ids_ref, small_sems.at[1])
    gain_copy.start()
    for step in range(tokens // tile):
        for copy in copies(step):
            copy.start()
        if step == 0:
            ids_copy.start()
    gain_copy.wait()

    def mean(partial):
        return jnp.sum(partial, axis=1, keepdims=True) * (1.0 / width)

    @pl.loop(0, tokens // tile)
    def _(step):
        for copy in copies(step):
            copy.wait()
        here = part(step)
        sum_value, sum_scaled = zero, zero
        for k, lanes in enumerate(columns):
            value = saved[here, lanes].astype(F32)
            scale = upstream[here, lanes].astype(F32) * gain_ref[k : k + 1, :]
            values[here, lanes] = value
            scaled[here, lanes] = scale
            sum_value += value
            sum_scaled += scale
        row_mean = jnp.broadcast_to(mean(sum_value), (tile, LANES))
        square, cross = zero, zero
        for lanes in columns:
            centered = values[here, lanes] - row_mean
            square += centered * centered
            cross += centered * scaled[here, lanes]
        inv_std = lax.rsqrt(mean(square) + 1e-05)
        along = inv_std * inv_std * inv_std * mean(cross)
        shift = inv_std * mean(sum_scaled)
        for i, stat in enumerate((row_mean, inv_std, along, shift)):
            stats[i, here, :] = jnp.broadcast_to(stat, (tile, LANES))

    row_mean, inv_std, along, shift = (stats[i] for i in range(4))
    ids_copy.wait()
    groups = LANES // capacity
    slots = owners * capacity
    slice_width = width // n_dp
    quarter = slice_width // groups
    block = stacked.shape[0] // (n_dp * (owners // groups))
    ids = ids_ref[...]
    owner = jnp.zeros_like(ids)
    for k in range(1, owners):
        owner = owner + (ids >= k * rows_owned).astype(jnp.int32)
    local = ids - owner * rows_owned
    down = lax.broadcasted_iota(jnp.int32, (tokens, tokens), 0)
    across = lax.broadcasted_iota(jnp.int32, (tokens, tokens), 1)
    column = lambda v: jnp.sum(
        jnp.where(down == across, jnp.broadcast_to(v.astype(F32), (tokens, tokens)), 0.0),
        axis=1,
        keepdims=True,
    )
    owner_col = column(owner)
    local_col = column(local)
    earlier = (owner.astype(F32) == owner_col) & (across < down)
    rank = jnp.sum(earlier.astype(F32), axis=1, keepdims=True)
    target = (owner_col * capacity + rank).astype(jnp.int32)
    placed = target == lax.broadcasted_iota(jnp.int32, (tokens, slots), 1)
    slot_of = placed.astype(F32).astype(BF16)
    slots_ref[...] = slot_of
    slot_id = (
        jnp.sum(jnp.where(placed, local_col + 1.0, 0.0), axis=0, keepdims=True).astype(
            jnp.int32
        )
        - 1
    )
    high = lax.shift_right_arithmetic(slot_id, base)
    low = slot_id - lax.shift_left(high, base)
    high, low = high.astype(F32), low.astype(F32)
    for lanes in columns:
        grad = inv_std * scaled[:, lanes] - shift - along * (values[:, lanes] - row_mean)
        turned[lanes, :] = dot(grad.astype(BF16), slot_of, ((0,), (0,)))
    tail = block - quarter
    for q in range(owners // groups):
        lanes = slice(q * LANES, (q + 1) * LANES)
        for d in range(n_dp):
            at = (q * n_dp + d) * block
            for j in range(groups):
                start = d * slice_width + j * quarter
                part = turned[start : start + quarter, lanes]
                extra = (high, low)[j][:, lanes] if j < 2 else jnp.zeros((1, LANES), F32)
                full = jnp.concatenate(
                    [part, jnp.broadcast_to(extra, (tail, LANES))], axis=0
                ).astype(BF16)
                stacked[at : at + block, j * LANES : (j + 1) * LANES] = full
    swapped = dot(stacked[...], swap_matrix(groups, capacity), ((1,), (0,))).astype(BF16)
    sent = out_ref.shape[1]
    for q in range(owners // groups):
        for d in range(n_dp):
            at = (q * n_dp + d) * block
            for b in range(groups):
                out_ref[d * owners + q * groups + b] = swapped[
                    at : at + sent, b * LANES : (b + 1) * LANES
                ]


def adam(old, first, second):
    fixed = second * (1.0 / (1.0 - 0.999**10))
    scale = fixed * lax.rsqrt(fixed) + 1e-08
    return old - (0.05 / (1.0 - 0.9**10)) * first / scale


def update_kernel(
    dims,
    arrived_ref,
    master,
    one,
    old_two_hbm,
    out_ref,
    master_hbm,
    one_hbm,
    two_hbm,
    total,
    stacked,
    turned,
    hot,
    table,
    two,
    master_new,
    one_new,
    two_new,
    sems,
    load_sem,
):
    capacity, base = dims
    groups = LANES // capacity
    sources, sent, _ = arrived_ref.shape
    slice_width, rows_owned = master.shape
    quarter = slice_width // groups
    tiles = sources // groups
    block = stacked.shape[0] // tiles
    span = 2 * LANES
    load = pltpu.make_async_copy(old_two_hbm, two, load_sem)
    load.start()
    swap = swap_matrix(groups, capacity)
    for a in range(tiles):
        for b in range(groups):
            stacked[a * block : a * block + sent, b * LANES : (b + 1) * LANES] = arrived_ref[
                a * groups + b
            ]
    down = lax.broadcasted_iota(jnp.int16, (rows_owned, LANES), 0)
    one_of, none_of = jnp.ones((rows_owned, LANES), BF16), jnp.zeros((rows_owned, LANES), BF16)
    id_row = sent - 1
    for a in range(tiles):
        lanes = slice(a * LANES, (a + 1) * LANES)
        swapped = dot(stacked[a * block : (a + 1) * block, :], swap, ((1,), (0,)))
        for j in range(groups):
            turned[j * block : (j + 1) * block, lanes] = swapped[
                :, j * LANES : (j + 1) * LANES
            ].astype(BF16)
        high = swapped[id_row : id_row + 1, 0:LANES].astype(jnp.int32)
        low = swapped[id_row : id_row + 1, LANES : 2 * LANES].astype(jnp.int32)
        ids = (lax.shift_left(high, base) + low).astype(jnp.int16)
        hot[:, lanes] = jnp.where(down == ids, one_of, none_of)

    def gather_rows(j, n):
        lanes = slice(n * span, (n + 1) * span)
        total[j * block : (j + 1) * block, lanes] = dot(
            turned[j * block : (j + 1) * block, :], hot[lanes, :], ((1,), (1,))
        )

    def step_rows(j, lanes):
        for top in range(0, quarter, 16):
            size = min(16, quarter - top)
            rows = slice(j * quarter + top, j * quarter + top + size)
            grad = total[j * block + top : j * block + top + size, lanes]
            first = 0.9 * one[rows, lanes] + 0.1 * grad
            second = 0.999 * two[rows, lanes] + 0.001 * grad * grad
            new = adam(0.995 * master[rows, lanes], first, second)
            one_new[rows, lanes] = first
            two_new[rows, lanes] = second
            master_new[rows, lanes] = new
            if size < 16:
                new = jnp.concatenate([new, jnp.zeros((16 - size, LANES), F32)], axis=0)
            table[j * block + top : j * block + top + 16, lanes] = new.astype(BF16)

    def look_rows(j, n):
        looked = dot(
            table[j * block : (j + 1) * block, :],
            hot[:, n * span : (n + 1) * span],
            ((1,), (0,)),
        ).astype(BF16)
        for h in range(2):
            at = (2 * n + h) * block
            stacked[at : at + block, j * LANES : (j + 1) * LANES] = looked[
                :, h * LANES : (h + 1) * LANES
            ]

    pieces = sems.shape[1]
    height = slice_width // pieces
    stores = [
        [
            pltpu.make_async_copy(
                held.at[p * height : (p + 1) * height], hbm.at[p * height : (p + 1) * height], sems.at[i, p]
            )
            for i, (held, hbm) in enumerate(
                ((master_new, master_hbm), (one_new, one_hbm), (two_new, two_hbm))
            )
        ]
        for p in range(pieces)
    ]
    load.wait()
    for n in range(rows_owned // span):
        gather_rows(0, n)
    for j in range(groups + 1):
        for n in range(max(rows_owned // span, tiles // 2)):
            if j + 1 < groups and n < rows_owned // span:
                gather_rows(j + 1, n)
            if j > 0 and n < tiles // 2:
                look_rows(j - 1, n)
            if j < groups and n < rows_owned // span:
                for h in range(2):
                    step_rows(j, slice((2 * n + h) * LANES, (2 * n + h + 1) * LANES))
        if groups - pieces <= j < groups:
            for copy in stores[j - groups + pieces]:
                copy.start()
    for a in range(tiles):
        back = dot(stacked[a * block : (a + 1) * block, :], swap, ((1,), (0,))).astype(BF16)
        for b in range(groups):
            out_ref[a * groups + b] = back[:quarter, b * LANES : (b + 1) * LANES]
    for piece in stores:
        for copy in piece:
            copy.wait()


def place_kernel(dims, rows_ref, slots_ref, out_ref, stacked, turned):
    n_dp, owners, capacity = dims
    groups = LANES // capacity
    quarter = rows_ref.shape[1]
    width = out_ref.shape[1]
    slice_width = width // n_dp
    block = stacked.shape[0] // (n_dp * (owners // groups))
    for q in range(owners // groups):
        for d in range(n_dp):
            at = (q * n_dp + d) * block
            for b in range(groups):
                stacked[at : at + quarter, b * LANES : (b + 1) * LANES] = rows_ref[
                    d * owners + q * groups + b
                ]
    swapped = dot(stacked[...], swap_matrix(groups, capacity), ((1,), (0,)))
    for q in range(owners // groups):
        for d in range(n_dp):
            at = (q * n_dp + d) * block
            for j in range(groups):
                start = d * slice_width + j * quarter
                turned[start : start + quarter, q * LANES : (q + 1) * LANES] = swapped[
                    at : at + quarter, j * LANES : (j + 1) * LANES
                ]
    for k in range(0, width, 2 * LANES):
        lanes = slice(k, min(k + 2 * LANES, width))
        out_ref[:, lanes] = dot(
            slots_ref[...], turned[lanes, :].astype(BF16), ((1,), (1,))
        ).astype(BF16)


def per_device(token_ids, upstream, saved_rows, norm_gain, master, moment_one, moment_two):
    axes = ("dp", "rows")
    n_dp, owners = lax.axis_size("dp"), lax.axis_size("rows")
    devices = n_dp * owners
    _, tokens, width = upstream.shape
    rows_owned, slice_width = master.shape
    capacity = tokens // 4
    groups = LANES // capacity
    quarter = slice_width // groups
    sent = round_up(quarter, 8) + 8
    block = round_up(sent, 16)
    slots = owners * capacity
    stack = devices // groups * block
    tile = 16
    base = 7
    full = pl.BlockSpec(memory_space=pltpu.VMEM)

    def params(mib):
        if devices * capacity > rows_owned:
            mib = 60
        return pltpu.CompilerParams(vmem_limit_bytes=mib * 2**20)

    hbm = pl.BlockSpec(memory_space=pltpu.HBM)
    blocks, slot_of = pl.pallas_call(
        functools.partial(send_kernel, (n_dp, owners, rows_owned, capacity, base)),
        in_specs=[hbm] * 4,
        out_specs=[full] * 2,
        out_shape=[
            jax.ShapeDtypeStruct((devices, sent, LANES), BF16),
            jax.ShapeDtypeStruct((tokens, slots), BF16),
        ],
        scratch_shapes=[
            pltpu.VMEM((1, tokens), jnp.int32),
            pltpu.VMEM((width // LANES, LANES), F32),
            pltpu.VMEM((tokens, width), BF16),
            pltpu.VMEM((tokens, width), BF16),
            pltpu.VMEM((tokens, width), F32),
            pltpu.VMEM((tokens, width), F32),
            pltpu.VMEM((4, tokens, LANES), F32),
            pltpu.VMEM((width, slots), F32),
            pltpu.VMEM((stack, groups * LANES), BF16),
            pltpu.SemaphoreType.DMA((2, tokens // tile)),
            pltpu.SemaphoreType.DMA((2,)),
        ],
        compiler_params=params(20),
        name="send",
    )(
        *(
            pltpu.with_memory_space_constraint(x, pltpu.HBM)
            for x in (
                token_ids,
                upstream[0],
                saved_rows[0],
                norm_gain.reshape(width // LANES, LANES),
            )
        )
    )
    arrived = lax.all_to_all(blocks, axes, split_axis=0, concat_axis=0, tiled=True)
    state = jax.ShapeDtypeStruct((slice_width, rows_owned), F32)
    slab = (master.T, moment_one.T, moment_two.T)
    found, master_new, one_new, two_new = pl.pallas_call(
        functools.partial(update_kernel, (capacity, base)),
        in_specs=[full] * 3 + [hbm],
        out_specs=[full] + [hbm] * 3,
        out_shape=[jax.ShapeDtypeStruct((devices, quarter, LANES), BF16)] + [state] * 3,
        scratch_shapes=[
            pltpu.VMEM((groups * block, rows_owned), F32),
            pltpu.VMEM((stack, groups * LANES), BF16),
            pltpu.VMEM((groups * block, devices * capacity), BF16),
            pltpu.VMEM((rows_owned, devices * capacity), BF16),
            pltpu.VMEM((groups * block, rows_owned), BF16),
            pltpu.VMEM(state.shape, F32),
            pltpu.VMEM(state.shape, F32),
            pltpu.VMEM(state.shape, F32),
            pltpu.VMEM(state.shape, F32),
            pltpu.SemaphoreType.DMA((3, groups if quarter % 8 == 0 else 1)),
            pltpu.SemaphoreType.DMA,
        ],
        compiler_params=params(28),
        name="update",
    )(arrived, slab[0], slab[1], pltpu.with_memory_space_constraint(slab[2], pltpu.HBM))
    rows = lax.all_to_all(found, axes, split_axis=0, concat_axis=0, tiled=True)
    new_rows = pl.pallas_call(
        functools.partial(place_kernel, (n_dp, owners, capacity)),
        in_specs=[full, full],
        out_specs=full,
        out_shape=jax.ShapeDtypeStruct((tokens, width), BF16),
        scratch_shapes=[
            pltpu.VMEM((stack, groups * LANES), BF16),
            pltpu.VMEM((width, slots), F32),
        ],
        compiler_params=params(16),
        name="place",
    )(rows, slot_of)
    return (master_new.T, one_new.T, two_new.T, new_rows[None])


def solution(mesh):
    split = P(("dp", "rows"), None, None)
    slab = P("rows", "dp")
    return jax.shard_map(
        per_device,
        mesh=mesh,
        in_specs=(P(("dp", "rows"), None), split, split, P(), slab, slab, slab),
        out_specs=(slab, slab, slab, split),
        check_vma=False,
    )
```

```python
import functools

import jax
import jax.numpy as jnp
from jax import lax
from jax.experimental import pallas as pl
from jax.experimental.pallas import tpu as pltpu
from jax.sharding import PartitionSpec as P

LANES = 128
F32 = jnp.float32
BF16 = jnp.bfloat16


def round_up(n, m):
    return (n + m - 1) // m * m


def dot(a, b, dims):
    return lax.dot_general(a, b, (dims, ((), ())), preferred_element_type=F32)


def swap_matrix(groups, width):
    size = groups * groups * width
    row = lax.broadcasted_iota(jnp.int32, (size, size), 0)
    col = lax.broadcasted_iota(jnp.int32, (1, size), 1)
    first = lax.div(col, groups * width)
    rest = col - first * (groups * width)
    second = lax.div(rest, width)
    target = second * (groups * width) + first * width + (rest - second * width)
    return (row == target).astype(F32).astype(BF16)


def send_kernel(
    dims,
    ids_hbm,
    upstream_hbm,
    saved_hbm,
    gain_hbm,
    out_ref,
    slots_ref,
    ids_ref,
    gain_ref,
    upstream,
    saved,
    values,
    scaled,
    stats,
    turned,
    stacked,
    sems,
    small_sems,
):
    n_dp, owners, rows_owned, capacity, base = dims
    tokens, width = values.shape
    tile = tokens // sems.shape[1]
    columns = [slice(k * LANES, (k + 1) * LANES) for k in range(width // LANES)]
    zero = jnp.zeros((tile, LANES), F32)

    def part(step):
        return pl.ds(pl.multiple_of(step * tile, tile), tile)

    def copies(step):
        return (
            pltpu.make_async_copy(saved_hbm.at[part(step)], saved.at[part(step)], sems.at[0, step]),
            pltpu.make_async_copy(
                upstream_hbm.at[part(step)], upstream.at[part(step)], sems.at[1, step]
            ),
        )

    gain_copy = pltpu.make_async_copy(gain_hbm, gain_ref, small_sems.at[0])
    ids_copy = pltpu.make_async_copy(ids_hbm, ids_ref, small_sems.at[1])
    gain_copy.start()
    for step in range(tokens // tile):
        for copy in copies(step):
            copy.start()
        if step == 0:
            ids_copy.start()
    gain_copy.wait()

    def mean(partial):
        return jnp.sum(partial, axis=1, keepdims=True) * (1.0 / width)

    @pl.loop(0, tokens // tile)
    def _(step):
        for copy in copies(step):
            copy.wait()
        here = part(step)
        sum_value, sum_scaled = zero, zero
        for k, lanes in enumerate(columns):
            value = saved[here, lanes].astype(F32)
            scale = upstream[here, lanes].astype(F32) * gain_ref[k : k + 1, :]
            values[here, lanes] = value
            scaled[here, lanes] = scale
            sum_value += value
            sum_scaled += scale
        row_mean = jnp.broadcast_to(mean(sum_value), (tile, LANES))
        square, cross = zero, zero
        for lanes in columns:
            centered = values[here, lanes] - row_mean
            square += centered * centered
            cross += centered * scaled[here, lanes]
        inv_std = lax.rsqrt(mean(square) + 1e-05)
        along = inv_std * inv_std * inv_std * mean(cross)
        shift = along * row_mean - inv_std * mean(sum_scaled)
        for i, stat in enumerate((inv_std, along, shift)):
            stats[i, here, :] = jnp.broadcast_to(stat, (tile, LANES))

    ids_copy.wait()
    groups = LANES // capacity
    slots = owners * capacity
    slice_width = width // n_dp
    quarter = slice_width // groups
    block = stacked.shape[0] // (n_dp * (owners // groups))
    ids = ids_ref[...]
    owner = jnp.zeros_like(ids)
    for k in range(1, owners):
        owner = owner + (ids >= k * rows_owned).astype(jnp.int32)
    local = ids - owner * rows_owned
    down = lax.broadcasted_iota(jnp.int32, (tokens, tokens), 0)
    across = lax.broadcasted_iota(jnp.int32, (tokens, tokens), 1)
    column = lambda v: jnp.sum(
        jnp.where(down == across, jnp.broadcast_to(v.astype(F32), (tokens, tokens)), 0.0),
        axis=1,
        keepdims=True,
    )
    owner_col = column(owner)
    local_col = column(local)
    earlier = (owner.astype(F32) == owner_col) & (across < down)
    rank = jnp.sum(earlier.astype(F32), axis=1, keepdims=True)
    target = (owner_col * capacity + rank).astype(jnp.int32)
    placed = target == lax.broadcasted_iota(jnp.int32, (tokens, slots), 1)
    slot_of = placed.astype(F32).astype(BF16)
    slots_ref[...] = slot_of
    slot_id = (
        jnp.sum(jnp.where(placed, local_col + 1.0, 0.0), axis=0, keepdims=True).astype(
            jnp.int32
        )
        - 1
    )
    high = lax.shift_right_arithmetic(slot_id, base)
    low = slot_id - lax.shift_left(high, base)
    high, low = high.astype(F32), low.astype(F32)
    tail = block - quarter
    sent = out_ref.shape[1]
    swap = swap_matrix(groups, capacity)
    ready, chunk = 0, 4
    for first in range(0, n_dp, chunk):
        while ready * LANES < (first + chunk) * slice_width:
            lanes = columns[ready]
            grad = stats[0] * scaled[:, lanes] - stats[1] * values[:, lanes] + stats[2]
            turned[lanes, :] = dot(grad.astype(BF16), slot_of, ((0,), (0,)))
            ready += 1
        for q in range(owners // groups):
            lanes = slice(q * LANES, (q + 1) * LANES)
            base_at = (q * n_dp + first) * block
            for d in range(chunk):
                at = base_at + d * block
                for j in range(groups):
                    start = (first + d) * slice_width + j * quarter
                    part = turned[start : start + quarter, lanes]
                    extra = (high, low)[j][:, lanes] if j < 2 else jnp.zeros((1, LANES), F32)
                    full = jnp.concatenate([part, jnp.broadcast_to(extra, (tail, LANES))], axis=0)
                    stacked[at : at + block, j * LANES : (j + 1) * LANES] = full.astype(BF16)
            swapped = dot(
                stacked[base_at : base_at + chunk * block, :], swap, ((1,), (0,))
            ).astype(BF16)
            for d in range(chunk):
                for b in range(groups):
                    out_ref[(first + d) * owners + q * groups + b] = swapped[
                        d * block : d * block + sent, b * LANES : (b + 1) * LANES
                    ]


def adam(old, first, second):
    second_fix = (1.0 - 0.999**10) ** 0.5
    scale = second * lax.rsqrt(second) + 1e-08 * second_fix
    return old - (0.05 / (1.0 - 0.9**10) * second_fix) * first / scale


def side_by_side(ref, first, count, groups):
    return jnp.concatenate(
        [
            jnp.concatenate([ref[a * groups + b] for b in range(groups)], axis=1)
            for a in range(first, first + count)
        ],
        axis=0,
    )


def update_kernel(
    dims,
    arrived_ref,
    master,
    one,
    old_two_hbm,
    out_ref,
    master_hbm,
    one_hbm,
    two_hbm,
    total,
    stacked,
    turned,
    hot,
    table,
    two,
    master_new,
    one_new,
    two_new,
    sems,
    load_sem,
):
    capacity, base = dims
    groups = LANES // capacity
    sources, sent, _ = arrived_ref.shape
    slice_width, rows_owned = master.shape
    quarter = slice_width // groups
    tiles = sources // groups
    block = stacked.shape[0] // tiles
    span = 2 * LANES
    load = pltpu.make_async_copy(old_two_hbm, two, load_sem)
    load.start()
    swap = swap_matrix(groups, capacity)
    down = lax.broadcasted_iota(jnp.int16, (rows_owned, LANES), 0)
    one_of, none_of = jnp.ones((rows_owned, LANES), BF16), jnp.zeros((rows_owned, LANES), BF16)
    id_row = sent - 1
    for c in range(0, tiles, 4):
        swapped = dot(side_by_side(arrived_ref, c, 4, groups), swap, ((1,), (0,)))
        for a in range(4):
            lanes = slice((c + a) * LANES, (c + a + 1) * LANES)
            at = a * sent
            for j in range(groups):
                turned[j * block : j * block + sent, lanes] = swapped[
                    at : at + sent, j * LANES : (j + 1) * LANES
                ].astype(BF16)
            ids_at = slice(at + id_row, at + id_row + 1)
            high = swapped[ids_at, 0:LANES].astype(jnp.int32)
            low = swapped[ids_at, LANES : 2 * LANES].astype(jnp.int32)
            ids = (lax.shift_left(high, base) + low).astype(jnp.int16)
            hot[:, lanes] = jnp.where(down == ids, one_of, none_of)

    bands = 2
    wide = groups // bands

    def band(i):
        return slice(i * wide * block, (i + 1) * wide * block)

    def gather_rows(i, n):
        lanes = slice(n * span, (n + 1) * span)
        total[band(i), lanes] = dot(turned[band(i), :], hot[lanes, :], ((1,), (1,)))

    def step_rows(j, lanes):
        for top in range(0, quarter, 16):
            size = min(16, quarter - top)
            rows = slice(j * quarter + top, j * quarter + top + size)
            grad = total[j * block + top : j * block + top + size, lanes]
            first = 0.9 * one[rows, lanes] + 0.1 * grad
            second = 0.999 * two[rows, lanes] + 0.001 * grad * grad
            new = adam(0.995 * master[rows, lanes], first, second)
            one_new[rows, lanes] = first
            two_new[rows, lanes] = second
            master_new[rows, lanes] = new
            if size < 16:
                new = jnp.concatenate([new, jnp.zeros((16 - size, LANES), F32)], axis=0)
            table[j * block + top : j * block + top + 16, lanes] = new.astype(BF16)

    def look_rows(i, n):
        lanes = slice(n * span, (n + 1) * span)
        looked = dot(table[band(i), :], hot[:, lanes], ((1,), (0,))).astype(BF16)
        for j in range(wide):
            for h in range(2):
                at, to = (2 * n + h) * block, (i * wide + j) * LANES
                stacked[at : at + block, to : to + LANES] = looked[
                    j * block : (j + 1) * block, h * LANES : (h + 1) * LANES
                ]

    pieces = sems.shape[1]
    height = slice_width // pieces
    stores = [
        [
            pltpu.make_async_copy(
                held.at[p * height : (p + 1) * height], hbm.at[p * height : (p + 1) * height], sems.at[i, p]
            )
            for i, (held, hbm) in enumerate(
                ((master_new, master_hbm), (one_new, one_hbm), (two_new, two_hbm))
            )
        ]
        for p in range(pieces)
    ]
    load.wait()
    steps = rows_owned // span
    looks = tiles // 2
    for n in range(steps):
        gather_rows(0, n)
    for i in range(bands + 1):
        for n in range(max(steps, looks)):
            if i + 1 < bands and n < steps:
                gather_rows(i + 1, n)
            if i > 0 and n < looks:
                look_rows(i - 1, n)
            if i < bands and n < steps:
                for h in range(2):
                    for j in range(i * wide, (i + 1) * wide):
                        step_rows(j, slice((2 * n + h) * LANES, (2 * n + h + 1) * LANES))
        if bands - pieces <= i < bands:
            for copy in stores[i - bands + pieces]:
                copy.start()
    for c in range(0, tiles, 4):
        back = dot(stacked[c * block : (c + 4) * block, :], swap, ((1,), (0,))).astype(BF16)
        for a in range(4):
            for b in range(groups):
                out_ref[(c + a) * groups + b] = back[
                    a * block : a * block + quarter, b * LANES : (b + 1) * LANES
                ]
    for piece in stores:
        for copy in piece:
            copy.wait()


def place_kernel(dims, rows_ref, slots_ref, out_hbm, stacked, turned, placed, sems):
    n_dp, owners, capacity = dims
    groups = LANES // capacity
    quarter = rows_ref.shape[1]
    width = placed.shape[1]
    slice_width = width // n_dp
    block = stacked.shape[0] // (n_dp * (owners // groups))
    for q in range(owners // groups):
        for d in range(n_dp):
            at = (q * n_dp + d) * block
            for b in range(groups):
                stacked[at : at + quarter, b * LANES : (b + 1) * LANES] = rows_ref[
                    d * owners + q * groups + b
                ]
    swapped = dot(stacked[...], swap_matrix(groups, capacity), ((1,), (0,)))
    for q in range(owners // groups):
        for d in range(n_dp):
            at = (q * n_dp + d) * block
            for j in range(groups):
                start = d * slice_width + j * quarter
                turned[start : start + quarter, q * LANES : (q + 1) * LANES] = swapped[
                    at : at + quarter, j * LANES : (j + 1) * LANES
                ]
    pieces = sems.shape[0]
    span = width // pieces
    copies = [
        pltpu.make_async_copy(
            placed.at[:, p * span : (p + 1) * span],
            out_hbm.at[:, p * span : (p + 1) * span],
            sems.at[p],
        )
        for p in range(pieces)
    ]
    for p, copy in enumerate(copies):
        for k in range(p * span, (p + 1) * span, 2 * LANES):
            lanes = slice(k, min(k + 2 * LANES, (p + 1) * span))
            placed[:, lanes] = dot(
                slots_ref[...], turned[lanes, :].astype(BF16), ((1,), (1,))
            ).astype(BF16)
        copy.start()
    for copy in copies:
        copy.wait()


def per_device(token_ids, upstream, saved_rows, norm_gain, master, moment_one, moment_two):
    axes = ("dp", "rows")
    n_dp, owners = lax.axis_size("dp"), lax.axis_size("rows")
    devices = n_dp * owners
    _, tokens, width = upstream.shape
    rows_owned, slice_width = master.shape
    capacity = tokens // 4
    groups = LANES // capacity
    quarter = slice_width // groups
    sent = round_up(quarter, 8) + 8
    block = round_up(sent, 16)
    slots = owners * capacity
    stack = devices // groups * block
    tile = 32
    base = 7
    full = pl.BlockSpec(memory_space=pltpu.VMEM)

    def params(mib):
        if devices * capacity > rows_owned:
            mib = 60
        return pltpu.CompilerParams(vmem_limit_bytes=mib * 2**20)

    hbm = pl.BlockSpec(memory_space=pltpu.HBM)
    blocks, slot_of = pl.pallas_call(
        functools.partial(send_kernel, (n_dp, owners, rows_owned, capacity, base)),
        in_specs=[hbm] * 4,
        out_specs=[full] * 2,
        out_shape=[
            jax.ShapeDtypeStruct((devices, sent, LANES), BF16),
            jax.ShapeDtypeStruct((tokens, slots), BF16),
        ],
        scratch_shapes=[
            pltpu.VMEM((1, tokens), jnp.int32),
            pltpu.VMEM((width // LANES, LANES), F32),
            pltpu.VMEM((tokens, width), BF16),
            pltpu.VMEM((tokens, width), BF16),
            pltpu.VMEM((tokens, width), F32),
            pltpu.VMEM((tokens, width), F32),
            pltpu.VMEM((3, tokens, LANES), F32),
            pltpu.VMEM((width, slots), F32),
            pltpu.VMEM((stack, groups * LANES), BF16),
            pltpu.SemaphoreType.DMA((2, tokens // tile)),
            pltpu.SemaphoreType.DMA((2,)),
        ],
        compiler_params=params(20),
        name="send",
    )(
        *(
            pltpu.with_memory_space_constraint(x, pltpu.HBM)
            for x in (
                token_ids,
                upstream[0],
                saved_rows[0],
                norm_gain.reshape(width // LANES, LANES),
            )
        )
    )
    arrived = lax.all_to_all(blocks, axes, split_axis=0, concat_axis=0, tiled=True)
    state = jax.ShapeDtypeStruct((slice_width, rows_owned), F32)
    slab = (master.T, moment_one.T, moment_two.T)
    found, master_new, one_new, two_new = pl.pallas_call(
        functools.partial(update_kernel, (capacity, base)),
        in_specs=[full] * 3 + [hbm],
        out_specs=[full] + [hbm] * 3,
        out_shape=[jax.ShapeDtypeStruct((devices, quarter, LANES), BF16)] + [state] * 3,
        scratch_shapes=[
            pltpu.VMEM((groups * block, rows_owned), F32),
            pltpu.VMEM((stack, groups * LANES), BF16),
            pltpu.VMEM((groups * block, devices * capacity), BF16),
            pltpu.VMEM((rows_owned, devices * capacity), BF16),
            pltpu.VMEM((groups * block, rows_owned), BF16),
            pltpu.VMEM(state.shape, F32),
            pltpu.VMEM(state.shape, F32),
            pltpu.VMEM(state.shape, F32),
            pltpu.VMEM(state.shape, F32),
            pltpu.SemaphoreType.DMA((3, 2 if quarter % 4 == 0 else 1)),
            pltpu.SemaphoreType.DMA,
        ],
        compiler_params=params(28),
        name="update",
    )(arrived, slab[0], slab[1], pltpu.with_memory_space_constraint(slab[2], pltpu.HBM))
    rows = lax.all_to_all(found, axes, split_axis=0, concat_axis=0, tiled=True)
    new_rows = pl.pallas_call(
        functools.partial(place_kernel, (n_dp, owners, capacity)),
        in_specs=[full, full],
        out_specs=hbm,
        out_shape=jax.ShapeDtypeStruct((tokens, width), BF16),
        scratch_shapes=[
            pltpu.VMEM((stack, groups * LANES), BF16),
            pltpu.VMEM((width, slots), F32),
            pltpu.VMEM((tokens, width), BF16),
            pltpu.SemaphoreType.DMA((3,)),
        ],
        compiler_params=params(16),
        name="place",
    )(rows, slot_of)
    return (master_new.T, one_new.T, two_new.T, new_rows[None])


def solution(mesh):
    split = P(("dp", "rows"), None, None)
    slab = P("rows", "dp")
    return jax.shard_map(
        per_device,
        mesh=mesh,
        in_specs=(P(("dp", "rows"), None), split, split, P(), slab, slab, slab),
        out_specs=(slab, slab, slab, split),
        check_vma=False,
    )
```
